32 devices in a mesh: region: 8 (over z, core), head: 4 (over y, x).
Axes of the slice: x: 2, y: 2, z: 4, core: 2. Of those that a mesh axis runs over, the one named last changes fastest.
Arguments:
- fine_tokens: float32 [18432, 512], P(('region', 'head')), may hold values from -6 to 6
- fine_shift: int32 [1], replicated, may hold values from 1 to 143
- window_counts: int32 [32], P('region'), may hold values from 36 to 144
- fine_qkv: bfloat16 [512, 1536], replicated, may hold values from -4 to 4
- fine_proj: bfloat16 [512, 512], replicated, may hold values from -0.25 to 0.25
- fine_up: bfloat16 [512, 2048], replicated, may hold values from -0.25 to 0.25
- fine_down: bfloat16 [2048, 512], replicated, may hold values from -0.125 to 0.125
- merge_weight: bfloat16 [2048, 1024], replicated, may hold values from -0.125 to 0.125
- coarse_qkv: bfloat16 [1024, 3072], P('region', 'head'), may hold values from -4 to 4
- coarse_proj: bfloat16 [1024, 1024], P('head', 'region'), may hold values from -0.1875 to 0.1875
- coarse_up: bfloat16 [1024, 4096], P('region', 'head'), may hold values from -0.1875 to 0.1875
- coarse_down: bfloat16 [4096, 1024], P('head', 'region'), may hold values from -0.09375 to 0.09375
- expand_weight: bfloat16 [1024, 2048], replicated, may hold values from -0.1875 to 0.1875
- out_weight: bfloat16 [1024, 512], replicated, may hold values from -0.1875 to 0.1875
Outputs:
- fine_result: float32 [18432, 512], P(('region', 'head'))
The draws below stay inside these ranges and needn't reach their ends.
All inputs are finite; a program needn't handle non-finite values.
Results may differ from the reference program's by a relative error of at most 0.012.
Values may be sent and summed in bfloat16 or wider, within the bound.
A program may use at most 128 MiB of HBM per device.

```python
import jax
import jax.numpy as jnp
from jax import lax

C = 512
HD = 64
HF = 8
D2 = 1024
HC = 16
FFF = 2048
FFC = 4096
WIN = 144
NTOK = 18432
NCW = 32


def drawn_qkv(key, channels, head_count):
    base = jax.random.normal(jax.random.fold_in(key, 11), (channels, head_count, 3, HD), jnp.float32)
    base = jnp.clip(base, -4.0, 4.0) * channels ** (-0.5)
    base = jnp.clip(base, -4.0, 4.0)
    return base.reshape(channels, head_count * 3 * HD)


def draw_fine_qkv(key, part):
    return drawn_qkv(key, C, HF).astype(jnp.bfloat16)


def draw_coarse_qkv(key, part):
    return drawn_qkv(key, D2, HC).astype(jnp.bfloat16)


def place_ends(entries, key, smallest, top_value):
    spot = [jax.random.randint(jax.random.fold_in(key, axis), (), 0, length) for axis, length in enumerate(entries.shape)]
    widest = entries.shape.index(max(entries.shape))
    neighbour = spot[:widest] + [(spot[widest] + 1) % entries.shape[widest]] + spot[widest + 1:]
    return entries.at[tuple(spot)].set(smallest).at[tuple(neighbour)].set(top_value)


def levels(own_key, shape, shards, least, top_value):
    loudness = 1.0
    for axis_at, shards_of in shards:
        steps = jax.random.uniform(jax.random.fold_in(jax.random.fold_in(own_key, 6), axis_at), (shards_of,), jnp.float32, least / len(shards), top_value / len(shards))
        loudness = loudness * jnp.repeat(jnp.exp(steps), shape[axis_at] // shards_of).reshape((-1,) + (1,) * (len(shape) - 1 - axis_at))
    return loudness


def normal_values(key, shape, deviation, limit, cuts=(), kind=jnp.bfloat16):
    drawn = jax.random.normal(key, shape, jnp.float32) * deviation
    if len(cuts) > 0:
        drawn = levels(key, shape, cuts, -0.22, 0.18) * drawn
    return jnp.clip(drawn, min=-limit, max=limit).astype(kind)


def setup_inputs(seed: int = 0) -> dict:
    keys = jax.random.split(jax.random.key(seed), 15)
    fine_tokens = normal_values(keys[0], (NTOK, C), 1.0, 6.0, ((0, 32),), jnp.float32)
    fine_shift = jax.random.randint(keys[1], (1,), 1, WIN).astype(jnp.int32)
    window_counts = place_ends(jax.random.randint(keys[2], (NCW,), WIN // 4, WIN + 1), jax.random.fold_in(keys[2], 1), WIN // 4, WIN).astype(jnp.int32)
    fine_qkv = draw_fine_qkv(jax.random.fold_in(keys[14], 71), 0)
    fine_proj = normal_values(keys[4], (C, C), C ** -0.5, 0.25)
    fine_up = normal_values(keys[5], (C, FFF), C ** -0.5, 0.25)
    fine_down = normal_values(keys[6], (FFF, C), FFF ** -0.5, 0.125)
    merge_weight = normal_values(keys[7], (4 * C, D2), (4 * C) ** -0.5, 0.125)
    coarse_qkv = draw_coarse_qkv(jax.random.fold_in(keys[14], 71), 0)
    coarse_proj = normal_values(keys[9], (D2, D2), D2 ** -0.5, 0.1875, ((0, 4), (1, 8)))
    coarse_up = normal_values(keys[10], (D2, FFC), D2 ** -0.5, 0.1875, ((0, 8), (1, 4)))
    coarse_down = normal_values(keys[11], (FFC, D2), FFC ** -0.5, 0.09375, ((0, 4), (1, 8)))
    expand_weight = normal_values(keys[12], (D2, 4 * C), D2 ** -0.5, 0.1875)
    out_weight = normal_values(keys[13], (2 * C, C), (2 * C) ** -0.5, 0.1875)
    return dict(fine_tokens=fine_tokens, fine_shift=fine_shift, window_counts=window_counts, fine_qkv=fine_qkv, fine_proj=fine_proj, fine_up=fine_up, fine_down=fine_down, merge_weight=merge_weight, coarse_qkv=coarse_qkv, coarse_proj=coarse_proj, coarse_up=coarse_up, coarse_down=coarse_down, expand_weight=expand_weight, out_weight=out_weight)


def layer_norm(values):
    average = lax.optimization_barrier(jnp.mean(values, axis=-1, keepdims=True))
    centred = values - average
    spread = lax.optimization_barrier(jnp.mean(centred * centred, axis=-1, keepdims=True))
    return centred * lax.rsqrt(spread + 1e-05)

def window_attention(normed, qkv_weight, proj_weight, head_count, head_size, window, counts):
    row_count = normed.shape[0]
    packed = jnp.dot(normed, qkv_weight, preferred_element_type=jnp.float32).astype(jnp.bfloat16)
    packed = lax.optimization_barrier(packed)
    packed = packed.reshape(row_count // window, window, head_count, 3, head_size).astype(jnp.float32)
    queries = packed[:, :, :, 0]
    key_part = packed[:, :, :, 1]
    value_part = packed[:, :, :, 2]
    scores = jnp.einsum('wqhd,wkhd->whqk', queries, key_part) * head_size ** (-0.5)
    if counts is not None:
        position = jnp.arange(window, dtype=jnp.int32)
        visible = position[None, :] < counts[:, None]
        scores = jnp.where(visible[:, None, None, :], scores, -1e+30)
    row_max = lax.optimization_barrier(jnp.max(scores, axis=-1, keepdims=True))
    raised = jnp.exp(scores - row_max)
    weights = (raised / lax.optimization_barrier(jnp.sum(raised, axis=-1, keepdims=True))).astype(jnp.bfloat16)
    weights = lax.optimization_barrier(weights).astype(jnp.float32)
    blended = jnp.einsum('whqk,wkhd->wqhd', weights, value_part).astype(jnp.bfloat16)
    blended = blended.reshape(row_count, head_count * head_size)
    return jnp.dot(blended, proj_weight, preferred_element_type=jnp.float32)

def feed_forward(normed, up_weight, down_weight):
    hidden = jnp.dot(normed, up_weight, preferred_element_type=jnp.float32)
    hidden = jax.nn.gelu(hidden, approximate=False).astype(jnp.bfloat16)
    return jnp.dot(hidden, down_weight, preferred_element_type=jnp.float32)

def reference(fine_tokens, fine_shift, window_counts, fine_qkv, fine_proj, fine_up, fine_down, merge_weight, coarse_qkv, coarse_proj, coarse_up, coarse_down, expand_weight, out_weight):
    offset = fine_shift[0]
    normed = layer_norm(fine_tokens).astype(jnp.bfloat16)
    rolled = jnp.roll(normed, -offset, axis=0)
    attended = window_attention(rolled, fine_qkv, fine_proj, HF, HD, WIN, None)
    fine_mid = fine_tokens + jnp.roll(attended, offset, axis=0)
    fine_out = fine_mid + feed_forward(layer_norm(fine_mid).astype(jnp.bfloat16), fine_up, fine_down)
    merged = fine_out.reshape(fine_out.shape[0] // 4, 4 * fine_out.shape[1])
    grouped = layer_norm(merged).astype(jnp.bfloat16)
    coarse = jnp.dot(grouped, merge_weight, preferred_element_type=jnp.float32)
    coarse_norm = layer_norm(coarse).astype(jnp.bfloat16)
    coarse_mid = coarse + window_attention(coarse_norm, coarse_qkv, coarse_proj, HC, HD, WIN, window_counts)
    coarse_out = coarse_mid + feed_forward(layer_norm(coarse_mid).astype(jnp.bfloat16), coarse_up, coarse_down)
    expanded = jnp.dot(coarse_out.astype(jnp.bfloat16), expand_weight, preferred_element_type=jnp.float32).astype(jnp.bfloat16)
    spread_rows = expanded.reshape(fine_out.shape[0], fine_out.shape[1])
    joined = jnp.concatenate([fine_out.astype(jnp.bfloat16), spread_rows], axis=1)
    return jnp.dot(joined, out_weight, preferred_element_type=jnp.float32)
```

```python
import functools

import jax
import jax.numpy as jnp
from jax import lax
from jax.experimental import pallas as pl
from jax.experimental.pallas import tpu as pltpu
from jax.sharding import PartitionSpec as P

C = 512
HD = 64
HF = 8
WIN = 144
HEADS = HF
MESH = pl.DeviceIdType.MESH
F32 = jnp.float32
BF16 = jnp.bfloat16


def norm(values):
    average = jnp.mean(values, axis=-1, keepdims=True)
    centred = values - average
    spread = jnp.mean(centred * centred, axis=-1, keepdims=True)
    return centred * lax.rsqrt(spread + 1e-05)


def gelu(values):
    return 0.5 * values * (1.0 + lax.erf(values * (0.5**0.5)))


def dot(left, right):
    return jnp.dot(left, right, preferred_element_type=F32)


def flip(index, mask):
    result = index
    bit = 1
    while bit <= mask:
        if mask & bit:
            result = result + (1 - 2 * ((index // bit) % 2)) * bit
        bit *= 2
    return result


def attend(packed, head_count, count):
    blended = []
    for head in range(head_count):
        base = head * 3 * HD
        query = packed[:, base : base + HD]
        key = packed[:, base + HD : base + 2 * HD]
        value = packed[:, base + 2 * HD : base + 3 * HD]
        scores = lax.dot_general(
            query, key, (((1,), (1,)), ((), ())), preferred_element_type=F32
        ) * (HD**-0.5)
        if count is not None:
            place = lax.broadcasted_iota(jnp.int32, scores.shape, 1)
            scores = jnp.where(place < count, scores, -1e30)
        raised = jnp.exp(scores - jnp.max(scores, axis=-1, keepdims=True))
        weights = (raised / jnp.sum(raised, axis=-1, keepdims=True)).astype(BF16)
        blended.append(dot(weights, value).astype(BF16))
    return blended


def kernel(
    region_count, head_count,
    shift, counts, tokens, w_qkv, w_proj, w_up, w_down, w_merge,
    c_qkv, c_proj, c_up, c_down, w_expand, w_out,
    out,
    v_qkv, v_proj, v_up, v_down, v_merge, v_expand, v_out,
    g_qkv, g_proj, g_up, g_down,
    extended, rolled, packed, blended, fine, fine_bf, hidden, grouped,
    coarse, shared, c_packed, c_blended, sent_blend, got_blend, mid, c_hidden, parts, got_parts, spread, lanes,
    local_sem, halo_send, halo_recv, own_sem, z_send, w_recv, p_send, q_send, q_recv,
    a_send, a_recv, b_send, b_recv, m_send, m_recv, r_send, r_recv,
):
    region, head = lax.axis_index("region"), lax.axis_index("head")
    chips = region_count // 2
    chip, core = region // 2, region % 2
    rows = tokens.shape[0]
    blocks = rows // WIN
    flat = region * head_count + head
    total = region_count * head_count
    before, after = (flat + total - 1) % total, (flat + 1) % total
    before = (before // head_count, before % head_count)
    after = (after // head_count, after % head_count)
    partner = (chip * 2 + 1 - core, head)
    column = [(((chip + s) % chips) * 2 + core, head) for s in range(chips)]
    plane = [(region, flip(head, k)) for k in range(head_count)]

    barrier = pltpu.get_barrier_semaphore()
    greeted = [before, after, partner] + column[1:] + plane[1:]
    for device in greeted:
        pl.semaphore_signal(barrier, inc=1, device_id=device, device_id_type=MESH)

    own = []
    for at, (source, target) in enumerate(
        [(w_qkv, v_qkv), (w_proj, v_proj), (w_up, v_up), (w_down, v_down), (w_merge, v_merge),
         (w_expand, v_expand), (w_out, v_out)]
    ):
        copy = pltpu.make_async_copy(source, target, local_sem.at[at])
        copy.start()
        own.append(copy)

    shards = [c_proj, c_qkv, c_up, c_down]

    def slot(which, owner):
        if which == 0:
            return g_proj.at[head, owner]
        if which == 1:
            return g_qkv.at[pl.ds(owner * c_qkv.shape[0], c_qkv.shape[0])]
        if which == 2:
            return g_up.at[pl.ds(owner * c_up.shape[0], c_up.shape[0])]
        return g_down.at[owner]

    own_shards = []
    for which in range(4):
        copy = pltpu.make_async_copy(shards[which], slot(which, region), own_sem.at[which])
        copy.start()
        own_shards.append(copy)

    def remote(source, target, send, recv, device):
        return pltpu.make_async_remote_copy(
            src_ref=source, dst_ref=target, send_sem=send, recv_sem=recv,
            device_id=device, device_id_type=MESH,
        )

    extended[WIN : WIN + rows, :] = norm(tokens[...]).astype(BF16)
    pl.semaphore_wait(barrier, len(greeted))

    halo_left = remote(extended.at[pl.ds(WIN, WIN)], extended.at[pl.ds(WIN + rows, WIN)],
                       halo_send.at[0], halo_recv.at[0], before)
    halo_right = remote(extended.at[pl.ds(rows, WIN)], extended.at[pl.ds(0, WIN)],
                        halo_send.at[1], halo_recv.at[1], after)
    halo_left.start()
    halo_right.start()

    column_sends = []
    for which in range(4):
        for s in range(1, chips):
            copy = remote(shards[which], slot(which, region), z_send.at[which, s],
                          w_recv.at[which, region], column[s])
            copy.start()
            column_sends.append(copy)

    partner_sends = []

    def pass_on(which):
        for s in range(chips):
            owner = ((chip + s) % chips) * 2 + core
            if s == 0:
                own_shards[which].wait()
            else:
                remote(shards[which], slot(which, owner), z_send.at[which, s],
                       w_recv.at[which, owner], column[s]).wait_recv()
            copy = remote(slot(which, owner), slot(which, owner), p_send.at[which, s],
                          w_recv.at[which, owner], partner)
            copy.start()
            partner_sends.append(copy)

    def take_over(which):
        for s in range(chips):
            owner = ((chip + s) % chips) * 2 + 1 - core
            remote(slot(which, owner), slot(which, owner), p_send.at[which, s],
                   w_recv.at[which, owner], partner).wait_recv()

    offset = shift[0]
    at_row = lax.broadcasted_iota(jnp.int32, (WIN, 2 * WIN), 0)
    at_column = lax.broadcasted_iota(jnp.int32, (WIN, 2 * WIN), 1)
    forth = (at_column == at_row + offset).astype(F32).astype(BF16)
    back = (at_column == at_row + (WIN - offset)).astype(F32).astype(BF16)
    halo_left.wait()
    halo_right.wait()
    for j in range(blocks + 1):
        rolled[j * WIN : (j + 1) * WIN, :] = dot(
            forth, extended[j * WIN : (j + 2) * WIN, :]
        ).astype(BF16)
    own[0].wait()

    def project(i, carry):
        at = pl.ds(pl.multiple_of(i * 256, 256), 256)
        packed[:, at] = dot(rolled[...], v_qkv[:, at]).astype(BF16)
        return carry

    lax.fori_loop(0, packed.shape[1] // 256, project, 0)

    def window(j, carry):
        at = pl.ds(pl.multiple_of(j * WIN, WIN), WIN)
        for half in range(2):
            width = packed.shape[1] // 2
            parts_of = attend(packed[at, half * width : (half + 1) * width], HEADS // 2, None)
            blended[at, half * (C // 2) : (half + 1) * (C // 2)] = jnp.concatenate(parts_of, axis=1)
        return carry

    lax.fori_loop(0, blocks + 1, window, 0)
    own[1].wait()
    for j in range(blocks):
        at = slice(j * WIN, (j + 1) * WIN)
        rolled[at, :] = dot(back, blended[j * WIN : (j + 2) * WIN, :]).astype(BF16)
    fine[...] = tokens[...] + dot(rolled[:rows, :], v_proj[...])
    rolled[:rows, :] = norm(fine[...]).astype(BF16)

    pass_on(0)
    own[2].wait()

    def fine_hidden(i, carry):
        at = pl.ds(pl.multiple_of(i * 256, 256), 256)
        hidden[:, at] = gelu(dot(rolled[:rows, :], v_up[:, at])).astype(BF16)
        return carry

    chunks = hidden.shape[1] // 256
    lax.fori_loop(0, chunks, fine_hidden, 0)
    take_over(0)
    quarter = []
    for k in range(1, head_count):
        copy = remote(g_proj.at[head], g_proj.at[head], q_send.at[k], q_recv.at[k], plane[k])
        copy.start()
        quarter.append(copy)
    own[3].wait()

    def fine_sum(i, carry):
        at = pl.ds(pl.multiple_of(i * 256, 256), 256)
        fine[:, at] += dot(hidden[...], v_down[:, at])
        return carry

    lax.fori_loop(0, C // 256, fine_sum, 0)
    pass_on(1)

    group = w_merge.shape[0] // C
    cells = rows // group
    own[4].wait()
    members = []
    for c in range(C // 128):
        lanes[c] = fine[:, c * 128 : (c + 1) * 128]
    for k in range(group):
        pieces = [lanes[c, pl.ds(k, cells, stride=group), :] for c in range(C // 128)]
        member = jnp.concatenate(pieces, axis=1)
        fine_bf[k * cells : (k + 1) * cells, :] = member.astype(BF16)
        members.append(member)
    merged = jnp.concatenate(members, axis=1)
    grouped[...] = norm(merged).astype(BF16)
    width = coarse.shape[1]

    def merge(i, carry):
        at = pl.ds(pl.multiple_of(i * 256, 256), 256)
        coarse[:, at] = dot(grouped[...], v_merge[:, at])
        return carry

    lax.fori_loop(0, width // 256, merge, 0)
    shared[head] = norm(coarse[...]).astype(BF16)
    gathers = []
    for k in range(1, head_count):
        copy = remote(shared.at[head], shared.at[head], a_send.at[k], a_recv.at[k], plane[k])
        copy.start()
        gathers.append(copy)
    take_over(1)

    blends = []
    heads_here = g_qkv.shape[1] // (3 * HD)
    for k in range(head_count):
        target = plane[k][1]
        if k > 0:
            gathers[k - 1].wait_recv()
        c_packed[...] = dot(shared[target], g_qkv[...]).astype(BF16)
        parts_of = attend(c_packed[...], heads_here, counts[target])
        if k == 0:
            got_blend[head] = jnp.concatenate(parts_of, axis=1)
        else:
            sent_blend[k] = jnp.concatenate(parts_of, axis=1)
            copy = remote(sent_blend.at[k], got_blend.at[head], b_send.at[k], b_recv.at[k], plane[k])
            copy.start()
            blends.append(copy)
    pass_on(2)
    for copy in quarter:
        copy.wait_recv()
    for copy in blends:
        copy.wait_recv()
    for r in range(region_count):
        w = g_proj.shape[3]
        total_of = dot(got_blend[0], g_proj[0, r])
        for h in range(1, head_count):
            total_of += dot(got_blend[h], g_proj[h, r])
        mid[:, r * w : (r + 1) * w] = coarse[:, r * w : (r + 1) * w] + total_of

    for copy in gathers:
        copy.wait_send()
    c_blended[head] = norm(mid[...]).astype(BF16)
    seconds = []
    for k in range(1, head_count):
        copy = remote(c_blended.at[head], c_blended.at[head], m_send.at[k], m_recv.at[k], plane[k])
        copy.start()
        seconds.append(copy)
    take_over(2)
    pass_on(3)

    returns = []
    for k in range(head_count):
        target = plane[k][1]
        if k > 0:
            seconds[k - 1].wait_recv()

        def coarse_hidden(i, carry):
            at = pl.ds(pl.multiple_of(i * 256, 256), 256)
            c_hidden[:, at] = gelu(dot(c_blended[target], g_up[:, at])).astype(BF16)
            return carry

        lax.fori_loop(0, c_hidden.shape[1] // 256, coarse_hidden, 0)
        if k == 0:
            take_over(3)
        w = g_down.shape[2]
        for r in range(0, region_count, 2):
            pair = jnp.concatenate([g_down[r], g_down[r + 1]], axis=1)
            term = dot(c_hidden[...], pair)
            if k == 0:
                mid[:, r * w : (r + 2) * w] += term
            else:
                parts[k, :, r * w : (r + 2) * w] = term.astype(BF16)
        if k > 0:
            copy = remote(parts.at[k], got_parts.at[k], r_send.at[k], r_recv.at[k], plane[k])
            copy.start()
            returns.append(copy)
    own[5].wait()
    own[6].wait()
    for copy in returns:
        copy.wait_recv()
    result = mid[...]
    for k in range(1, head_count):
        result += got_parts[k].astype(F32)
    grouped[:, :width] = result.astype(BF16)
    for k in range(group):
        spread[k * cells : (k + 1) * cells, :] = dot(
            grouped[:, :width], v_expand[:, k * C : (k + 1) * C]
        ).astype(BF16)
    for c in range(C // 128):
        at = slice(c * 128, (c + 1) * 128)
        value = dot(fine_bf[...], v_out[:C, at]) + dot(spread[...], v_out[C:, at])
        for k in range(group):
            lanes[c, pl.ds(k, cells, stride=group), :] = value[k * cells : (k + 1) * cells, :]
        out[:, at] = lanes[c]

    for copy in column_sends + partner_sends + quarter + blends + seconds + returns:
        copy.wait_send()


def body(region_count, head_count, tokens, shift, counts, *weights):
    rows = tokens.shape[0]
    w_qkv, w_proj, w_up, w_down, w_merge, c_qkv, c_proj, c_up, c_down, w_expand, w_out = weights
    width = w_merge.shape[1]
    group = w_merge.shape[0] // C
    cells = rows // group
    vmem = pltpu.VMEM
    any_spec = pl.BlockSpec(memory_space=pl.ANY)
    dma = pltpu.SemaphoreType.DMA
    chips = region_count // 2
    mine = c_proj.shape[0]
    scratch = [vmem(w.shape, BF16) for w in (w_qkv, w_proj, w_up, w_down, w_merge, w_expand, w_out)]
    scratch += [
        vmem((width, c_qkv.shape[1]), BF16),
        vmem((head_count, region_count) + c_proj.shape, BF16),
        vmem((width, c_up.shape[1]), BF16),
        vmem((region_count,) + c_down.shape, BF16),
        vmem((rows + 2 * WIN, C), BF16),
        vmem((rows + WIN, C), BF16),
        vmem((rows + WIN, w_qkv.shape[1]), BF16),
        vmem((rows + WIN, C), BF16),
        vmem((rows, C), F32),
        vmem((rows, C), BF16),
        vmem((rows, w_up.shape[1]), BF16),
        vmem((cells, group * C), BF16),
        vmem((cells, width), F32),
        vmem((head_count, cells, width), BF16),
        vmem((cells, c_qkv.shape[1]), BF16),
        vmem((head_count, cells, width), BF16),
        vmem((head_count, cells, mine), BF16),
        vmem((head_count, cells, mine), BF16),
        vmem((cells, width), F32),
        vmem((cells, c_up.shape[1]), BF16),
        vmem((head_count, cells, width), BF16),
        vmem((head_count, cells, width), BF16),
        vmem((rows, C), BF16),
        vmem((C // 128, rows, 128), F32),
        dma((7,)), dma((2,)), dma((2,)), dma((4,)), dma((4, chips)), dma((4, region_count)), dma((4, chips)),
    ]
    scratch += [dma((head_count,)) for _ in range(10)]
    return pl.pallas_call(
        functools.partial(kernel, region_count, head_count),
        out_shape=jax.ShapeDtypeStruct((rows, C), F32),
        in_specs=[pl.BlockSpec(memory_space=pltpu.SMEM)] * 2
        + [pl.BlockSpec(memory_space=pltpu.VMEM)] + [any_spec] * 11,
        out_specs=pl.BlockSpec(memory_space=pltpu.VMEM),
        scratch_shapes=scratch,
        compiler_params=pltpu.CompilerParams(
            collective_id=0, has_side_effects=True, vmem_limit_bytes=60 * 1024 * 1024
        ),
    )(shift, counts, tokens, *weights)


def solution(mesh):
    in_specs = (
        P(("region", "head"), None), P(), P("region"), P(), P(), P(), P(), P(),
        P("region", "head"), P("head", "region"), P("region", "head"), P("head", "region"), P(), P(),
    )
    out_specs = P(("region", "head"), None)
    run = functools.partial(body, mesh.shape["region"], mesh.shape["head"])
    return jax.shard_map(run, mesh=mesh, in_specs=in_specs, out_specs=out_specs, check_vma=False)
```

```python
import functools

import jax
import jax.numpy as jnp
from jax import lax
from jax.experimental import pallas as pl
from jax.experimental.pallas import tpu as pltpu
from jax.sharding import PartitionSpec as P

C = 512
HD = 64
HF = 8
WIN = 144
HEADS = HF
MESH = pl.DeviceIdType.MESH
F32 = jnp.float32
BF16 = jnp.bfloat16


def norm(values):
    average = jnp.mean(values, axis=-1, keepdims=True)
    centred = values - average
    spread = jnp.mean(centred * centred, axis=-1, keepdims=True)
    return centred * lax.rsqrt(spread + 1e-05)


def gelu(values):
    return 0.5 * values * (1.0 + lax.erf(values * (0.5**0.5)))


def dot(left, right):
    return jnp.dot(left, right, preferred_element_type=F32)


def flip(index, mask):
    result = index
    bit = 1
    while bit <= mask:
        if mask & bit:
            result = result + (1 - 2 * ((index // bit) % 2)) * bit
        bit *= 2
    return result


def attend(packed, head_count, count):
    blended = []
    for head in range(head_count):
        base = head * 3 * HD
        query = packed[:, base : base + HD]
        key = packed[:, base + HD : base + 2 * HD]
        value = packed[:, base + 2 * HD : base + 3 * HD]
        scores = lax.dot_general(
            query, key, (((1,), (1,)), ((), ())), preferred_element_type=F32
        ) * (HD**-0.5)
        if count is not None:
            place = lax.broadcasted_iota(jnp.int32, scores.shape, 1)
            scores = jnp.where(place < count, scores, -1e30)
        raised = jnp.exp(scores - jnp.max(scores, axis=-1, keepdims=True))
        weights = (raised / jnp.sum(raised, axis=-1, keepdims=True)).astype(BF16)
        blended.append(dot(weights, value).astype(BF16))
    return blended


def kernel(
    region_count, head_count,
    shift, counts, tokens, w_qkv, w_proj, w_up, w_down, w_merge,
    c_qkv, c_proj, c_up, c_down, w_expand, w_out,
    out,
    v_qkv, v_proj, v_up, v_down, v_merge, v_expand, v_out,
    g_qkv, g_proj, g_up, g_down,
    extended, rolled, packed, blended, fine, fine_bf, hidden, grouped,
    coarse, shared, c_packed, c_blended, sent_blend, got_blend, mid, c_hidden, parts, got_parts, spread, lanes,
    local_sem, halo_send, halo_recv, own_sem, z_send, w_recv, p_send, q_send, q_recv, x_send, x_recv,
    a_send, a_recv, b_send, b_recv, m_send, m_recv, r_send, r_recv,
):
    region, head = lax.axis_index("region"), lax.axis_index("head")
    chips = region_count // 2
    chip, core = region // 2, region % 2
    rows = tokens.shape[0]
    blocks = rows // WIN
    flat = region * head_count + head
    total = region_count * head_count
    before, after = (flat + total - 1) % total, (flat + 1) % total
    before = (before // head_count, before % head_count)
    after = (after // head_count, after % head_count)
    partner = (chip * 2 + 1 - core, head)
    column = [(((chip + s) % chips) * 2 + core, head) for s in range(chips)]
    plane = [(region, flip(head, k)) for k in range(head_count)]

    barrier = pltpu.get_barrier_semaphore()
    greeted = [before, after, partner] + column[1:] + plane[1:]
    for device in greeted:
        pl.semaphore_signal(barrier, inc=1, device_id=device, device_id_type=MESH)

    own = []
    for at, (source, target) in enumerate(
        [(w_qkv, v_qkv), (w_proj, v_proj), (w_up, v_up), (w_down, v_down), (w_merge, v_merge),
         (w_expand, v_expand), (w_out, v_out)]
    ):
        copy = pltpu.make_async_copy(source, target, local_sem.at[at])
        copy.start()
        own.append(copy)

    shards = [c_proj, c_qkv, c_up, c_down]

    def slot(which, owner):
        if which == 0:
            return g_proj.at[head, owner]
        if which == 1:
            return g_qkv.at[pl.ds(owner * c_qkv.shape[0], c_qkv.shape[0])]
        if which == 2:
            return g_up.at[pl.ds(owner * c_up.shape[0], c_up.shape[0])]
        return g_down.at[owner]

    own_shards = []
    for which in range(4):
        copy = pltpu.make_async_copy(shards[which], slot(which, region), own_sem.at[which])
        copy.start()
        own_shards.append(copy)

    def remote(source, target, send, recv, device):
        return pltpu.make_async_remote_copy(
            src_ref=source, dst_ref=target, send_sem=send, recv_sem=recv,
            device_id=device, device_id_type=MESH,
        )

    extended[WIN : WIN + rows, :] = norm(tokens[...]).astype(BF16)
    pl.semaphore_wait(barrier, len(greeted))

    halo_left = remote(extended.at[pl.ds(WIN, WIN)], extended.at[pl.ds(WIN + rows, WIN)],
                       halo_send.at[0], halo_recv.at[0], before)
    halo_right = remote(extended.at[pl.ds(rows, WIN)], extended.at[pl.ds(0, WIN)],
                        halo_send.at[1], halo_recv.at[1], after)
    halo_left.start()
    halo_right.start()

    column_sends = []
    for which in range(4):
        for s in range(1, chips):
            copy = remote(shards[which], slot(which, region), z_send.at[which, s],
                          w_recv.at[which, region], column[s])
            copy.start()
            column_sends.append(copy)

    partner_sends = []

    def pass_on(which):
        for s in range(chips):
            owner = ((chip + s) % chips) * 2 + core
            if s == 0:
                own_shards[which].wait()
            else:
                remote(shards[which], slot(which, owner), z_send.at[which, s],
                       w_recv.at[which, owner], column[s]).wait_recv()
            copy = remote(slot(which, owner), slot(which, owner), p_send.at[which, s],
                          w_recv.at[which, owner], partner)
            copy.start()
            partner_sends.append(copy)

    def take_over(which):
        for s in range(chips):
            owner = ((chip + s) % chips) * 2 + 1 - core
            remote(slot(which, owner), slot(which, owner), p_send.at[which, s],
                   w_recv.at[which, owner], partner).wait_recv()

    relay = head_count == 4

    def gather(buffer, send, recv):
        copies = []
        for k in range(1, 3 if relay else head_count):
            piece = buffer.at[head]
            copy = remote(piece, piece, send.at[k], recv.at[k], plane[k])
            copy.start()
            copies.append(copy)
        return copies

    def far_half(buffer, mask, i, send, recv, device):
        half = buffer.shape[2] // 2
        piece = buffer.at[flip(head, mask), :, pl.ds(i * half, half)]
        return remote(piece, piece, send.at[3 * i], recv.at[3 * i], device)

    def hand_on(buffer, send, recv, copies):
        if not relay:
            return
        for i, (came, goes) in enumerate(((1, 2), (2, 1))):
            copies[came - 1].wait_recv()
            copy = far_half(buffer, came, i, send, recv, plane[goes])
            copy.start()
            copies.append(copy)

    def arrived(buffer, k, send, recv, copies):
        if not relay:
            copies[k - 1].wait_recv()
        elif k == 3:
            for i, came in enumerate((2, 1)):
                far_half(buffer, 3, i, send, recv, plane[came]).wait_recv()

    offset = shift[0]
    at_row = lax.broadcasted_iota(jnp.int32, (WIN, 2 * WIN), 0)
    at_column = lax.broadcasted_iota(jnp.int32, (WIN, 2 * WIN), 1)
    forth = (at_column == at_row + offset).astype(F32).astype(BF16)
    back = (at_column == at_row + (WIN - offset)).astype(F32).astype(BF16)
    halo_left.wait()
    halo_right.wait()
    for j in range(blocks + 1):
        rolled[j * WIN : (j + 1) * WIN, :] = dot(
            forth, extended[j * WIN : (j + 2) * WIN, :]
        ).astype(BF16)
    own[0].wait()

    def project(i, carry):
        at = pl.ds(pl.multiple_of(i * 256, 256), 256)
        packed[:, at] = dot(rolled[...], v_qkv[:, at]).astype(BF16)
        return carry

    lax.fori_loop(0, packed.shape[1] // 256, project, 0)
    pass_on(0)
    quarter = []
    for s in range(chips):
        owner = ((chip + s) % chips) * 2 + core
        for k in range(1, head_count):
            piece = g_proj.at[head, owner]
            copy = remote(piece, piece, q_send.at[k, s], q_recv.at[k, s], plane[k])
            copy.start()
            quarter.append(copy)

    def window(j, carry):
        at = pl.ds(pl.multiple_of(j * WIN, WIN), WIN)
        for half in range(2):
            width = packed.shape[1] // 2
            parts_of = attend(packed[at, half * width : (half + 1) * width], HEADS // 2, None)
            blended[at, half * (C // 2) : (half + 1) * (C // 2)] = jnp.concatenate(parts_of, axis=1)
        return carry

    lax.fori_loop(0, blocks + 1, window, 0)
    own[1].wait()
    for j in range(blocks):
        at = slice(j * WIN, (j + 1) * WIN)
        rolled[at, :] = dot(back, blended[j * WIN : (j + 2) * WIN, :]).astype(BF16)
    fine[...] = tokens[...] + dot(rolled[:rows, :], v_proj[...])
    rolled[:rows, :] = norm(fine[...]).astype(BF16)

    for s in range(chips):
        owner = ((chip + s) % chips) * 2 + core
        for k in range(1, head_count):
            piece = g_proj.at[plane[k][1], owner]
            remote(piece, piece, q_send.at[k, s], q_recv.at[k, s], plane[k]).wait_recv()
            copy = remote(piece, piece, x_send.at[k, s], x_recv.at[k, s], partner)
            copy.start()
            partner_sends.append(copy)
    own[2].wait()

    def fine_hidden(i, carry):
        at = pl.ds(pl.multiple_of(i * 256, 256), 256)
        hidden[:, at] = gelu(dot(rolled[:rows, :], v_up[:, at])).astype(BF16)
        return carry

    chunks = hidden.shape[1] // 256
    lax.fori_loop(0, chunks, fine_hidden, 0)
    own[3].wait()

    def fine_sum(i, carry):
        at = pl.ds(pl.multiple_of(i * 256, 256), 256)
        fine[:, at] += dot(hidden[...], v_down[:, at])
        return carry

    lax.fori_loop(0, C // 256, fine_sum, 0)
    pass_on(1)

    group = w_merge.shape[0] // C
    cells = rows // group
    own[4].wait()
    members = []
    for c in range(C // 128):
        lanes[c] = fine[:, c * 128 : (c + 1) * 128]
    for k in range(group):
        pieces = [lanes[c, pl.ds(k, cells, stride=group), :] for c in range(C // 128)]
        member = jnp.concatenate(pieces, axis=1)
        fine_bf[k * cells : (k + 1) * cells, :] = member.astype(BF16)
        members.append(member)
    merged = jnp.concatenate(members, axis=1)
    grouped[...] = norm(merged).astype(BF16)
    width = coarse.shape[1]

    def merge(i, carry):
        at = pl.ds(pl.multiple_of(i * 256, 256), 256)
        coarse[:, at] = dot(grouped[...], v_merge[:, at])
        return carry

    lax.fori_loop(0, width // 256, merge, 0)
    shared[head] = norm(coarse[...]).astype(BF16)
    gathers = gather(shared, a_send, a_recv)
    take_over(1)

    blends = []
    heads_here = g_qkv.shape[1] // (3 * HD)
    for k in range(head_count):
        target = plane[k][1]
        if k > 0:
            arrived(shared, k, a_send, a_recv, gathers)
        c_packed[...] = dot(shared[target], g_qkv[...]).astype(BF16)
        parts_of = attend(c_packed[...], heads_here, counts[target])
        if k == 0:
            got_blend[head] = jnp.concatenate(parts_of, axis=1)
            hand_on(shared, a_send, a_recv, gathers)
        else:
            sent_blend[k] = jnp.concatenate(parts_of, axis=1)
            copy = remote(sent_blend.at[k], got_blend.at[head], b_send.at[k], b_recv.at[k], plane[k])
            copy.start()
            blends.append(copy)
    pass_on(2)
    take_over(0)
    for s in range(chips):
        owner = ((chip + s) % chips) * 2 + 1 - core
        for k in range(1, head_count):
            piece = g_proj.at[plane[k][1], owner]
            remote(piece, piece, x_send.at[k, s], x_recv.at[k, s], partner).wait_recv()
    for copy in blends:
        copy.wait_recv()
    for r in range(region_count):
        w = g_proj.shape[3]
        total_of = dot(got_blend[0], g_proj[0, r])
        for h in range(1, head_count):
            total_of += dot(got_blend[h], g_proj[h, r])
        mid[:, r * w : (r + 1) * w] = coarse[:, r * w : (r + 1) * w] + total_of

    c_blended[head] = norm(mid[...]).astype(BF16)
    seconds = gather(c_blended, m_send, m_recv)
    take_over(2)
    pass_on(3)

    returns = []
    for k in range(head_count):
        target = plane[k][1]
        if k > 0:
            arrived(c_blended, k, m_send, m_recv, seconds)

        def coarse_hidden(i, carry):
            at = pl.ds(pl.multiple_of(i * 256, 256), 256)
            c_hidden[:, at] = gelu(dot(c_blended[target], g_up[:, at])).astype(BF16)
            return carry

        lax.fori_loop(0, c_hidden.shape[1] // 256, coarse_hidden, 0)
        if k == 0:
            hand_on(c_blended, m_send, m_recv, seconds)
            take_over(3)
        w = g_down.shape[2]
        for r in range(0, region_count, 2):
            pair = jnp.concatenate([g_down[r], g_down[r + 1]], axis=1)
            term = dot(c_hidden[...], pair)
            if k == 0:
                mid[:, r * w : (r + 2) * w] += term
            else:
                parts[k, :, r * w : (r + 2) * w] = term.astype(BF16)
        if k > 0:
            copy = remote(parts.at[k], got_parts.at[k], r_send.at[k], r_recv.at[k], plane[k])
            copy.start()
            returns.append(copy)
    own[5].wait()
    own[6].wait()
    for copy in returns:
        copy.wait_recv()
    result = mid[...]
    for k in range(1, head_count):
        result += got_parts[k].astype(F32)
    grouped[:, :width] = result.astype(BF16)
    for k in range(group):
        spread[k * cells : (k + 1) * cells, :] = dot(
            grouped[:, :width], v_expand[:, k * C : (k + 1) * C]
        ).astype(BF16)
    for c in range(C // 128):
        at = slice(c * 128, (c + 1) * 128)
        value = dot(fine_bf[...], v_out[:C, at]) + dot(spread[...], v_out[C:, at])
        for k in range(group):
            lanes[c, pl.ds(k, cells, stride=group), :] = value[k * cells : (k + 1) * cells, :]
        out[:, at] = lanes[c]

    for copy in column_sends + partner_sends + quarter + gathers + blends + seconds + returns:
        copy.wait_send()


def body(region_count, head_count, tokens, shift, counts, *weights):
    rows = tokens.shape[0]
    w_qkv, w_proj, w_up, w_down, w_merge, c_qkv, c_proj, c_up, c_down, w_expand, w_out = weights
    width = w_merge.shape[1]
    group = w_merge.shape[0] // C
    cells = rows // group
    vmem = pltpu.VMEM
    any_spec = pl.BlockSpec(memory_space=pl.ANY)
    dma = pltpu.SemaphoreType.DMA
    chips = region_count // 2
    mine = c_proj.shape[0]
    scratch = [vmem(w.shape, BF16) for w in (w_qkv, w_proj, w_up, w_down, w_merge, w_expand, w_out)]
    scratch += [
        vmem((width, c_qkv.shape[1]), BF16),
        vmem((head_count, region_count) + c_proj.shape, BF16),
        vmem((width, c_up.shape[1]), BF16),
        vmem((region_count,) + c_down.shape, BF16),
        vmem((rows + 2 * WIN, C), BF16),
        vmem((rows + WIN, C), BF16),
        vmem((rows + WIN, w_qkv.shape[1]), BF16),
        vmem((rows + WIN, C), BF16),
        vmem((rows, C), F32),
        vmem((rows, C), BF16),
        vmem((rows, w_up.shape[1]), BF16),
        vmem((cells, group * C), BF16),
        vmem((cells, width), F32),
        vmem((head_count, cells, width), BF16),
        vmem((cells, c_qkv.shape[1]), BF16),
        vmem((head_count, cells, width), BF16),
        vmem((head_count, cells, mine), BF16),
        vmem((head_count, cells, mine), BF16),
        vmem((cells, width), F32),
        vmem((cells, c_up.shape[1]), BF16),
        vmem((head_count, cells, width), BF16),
        vmem((head_count, cells, width), BF16),
        vmem((rows, C), BF16),
        vmem((C // 128, rows, 128), F32),
        dma((7,)), dma((2,)), dma((2,)), dma((4,)), dma((4, chips)), dma((4, region_count)), dma((4, chips)),
    ]
    scratch += [dma((head_count, chips)) for _ in range(4)]
    scratch += [dma((head_count,)) for _ in range(8)]
    return pl.pallas_call(
        functools.partial(kernel, region_count, head_count),
        out_shape=jax.ShapeDtypeStruct((rows, C), F32),
        in_specs=[pl.BlockSpec(memory_space=pltpu.SMEM)] * 2
        + [pl.BlockSpec(memory_space=pltpu.VMEM)] + [any_spec] * 11,
        out_specs=pl.BlockSpec(memory_space=pltpu.VMEM),
        scratch_shapes=scratch,
        compiler_params=pltpu.CompilerParams(
            collective_id=0, has_side_effects=True, vmem_limit_bytes=60 * 1024 * 1024
        ),
    )(shift, counts, tokens, *weights)


def solution(mesh):
    in_specs = (
        P(("region", "head"), None), P(), P("region"), P(), P(), P(), P(), P(),
        P("region", "head"), P("head", "region"), P("region", "head"), P("head", "region"), P(), P(),
    )
    out_specs = P(("region", "head"), None)
    run = functools.partial(body, mesh.shape["region"], mesh.shape["head"])
    return jax.shard_map(run, mesh=mesh, in_specs=in_specs, out_specs=out_specs, check_vma=False)
```
